128 devices in a mesh: tm: 16 (over x, y), tile: 8 (over z, core).
Axes of the slice: x: 4, y: 4, z: 4, core: 2. Of those that a mesh axis runs over, the one named last changes fastest.
Arguments:
- latent: bfloat16 [32, 32, 128, 16], P('tm', 'tile'), may hold values from -6 to 6
- cache_lat: bfloat16 [2, 32, 128, 16], P(None, 'tile'), may hold values from -6 to 6
- cache_one: bfloat16 [2, 32, 128, 384], P(None, 'tile'), may hold values from -6 to 6
- cache_two: bfloat16 [2, 32, 128, 384], P(None, 'tile'), may hold values from -6 to 6
- w_in: bfloat16 [3, 3, 3, 16, 384], replicated, may hold values from -0.3125 to 0.3125
- b_in: float32 [384], replicated, may hold values from -3 to 3
- gain_one: float32 [384], replicated, may hold values from 0.1 to 1.9
- w_one: bfloat16 [3, 3, 3, 384, 384], replicated, may hold values from -0.0625 to 0.0625
- b_one: float32 [384], replicated, may hold values from -3 to 3
- gain_two: float32 [384], replicated, may hold values from 0.1 to 1.9
- w_two: bfloat16 [3, 3, 3, 384, 384], replicated, may hold values from -0.0625 to 0.0625
- b_two: float32 [384], replicated, may hold values from -3 to 3
Outputs:
- decoded: bfloat16 [32, 32, 128, 384], P('tm', 'tile')
The draws below stay inside these ranges and needn't reach their ends.
All inputs are finite; a program needn't handle non-finite values.
Results may differ from the reference program's by a relative error of at most 0.0051.
Values may be sent and summed in bfloat16 or wider, within the bound.
A program may use at most 320 MiB of HBM per device.

```python
import jax
import jax.numpy as jnp
from jax import lax

CIN = 16
C = 384
WIDE = 128
TT = 32
HH = 32


def levels(rng, shape, split, least, largest):
    loudness, own = 1.0, jax.random.fold_in(rng, 6)
    for dim, parts in split:
        draws = jnp.exp(jax.random.uniform(jax.random.fold_in(own, dim), (parts,), jnp.float32, least / len(split), largest / len(split)))
        loudness = loudness * jnp.repeat(draws, shape[dim] // parts).reshape([-1 if axis == dim else 1 for axis in range(len(shape))])
    return loudness


def scatter_about(own_key, shape, scale, most, shards=(), held_as=jnp.bfloat16):
    drawn = scale * jax.random.normal(own_key, shape, jnp.float32)
    if shards:
        drawn = drawn * levels(own_key, shape, shards, -0.22, 0.18)
    return jnp.clip(drawn, -most, most).astype(held_as)


def setup_inputs(seed: int = 0) -> dict:
    arg_keys = jax.random.split(jax.random.key(seed), 13)
    latent = scatter_about(arg_keys[0], (TT, HH, WIDE, CIN), 1.0, 6.0, ((0, 16), (1, 8)))
    cache_lat = scatter_about(arg_keys[1], (2, HH, WIDE, CIN), 1.0, 6.0, ((1, 8),))
    cache_one = scatter_about(arg_keys[2], (2, HH, WIDE, C), 1.0, 6.0, ((1, 8),))
    cache_two = scatter_about(arg_keys[3], (2, HH, WIDE, C), 1.0, 6.0, ((1, 8),))
    w_in = scatter_about(arg_keys[4], (3, 3, 3, CIN, C), (27 * CIN) ** -0.5, 0.3125)
    b_in = scatter_about(arg_keys[5], (C,), 0.5, 3.0, (), jnp.float32)
    gain_one = jnp.clip(1.0 + 0.18 * jax.random.normal(arg_keys[6], (C,), jnp.float32), 0.1, 1.9)
    w_one = scatter_about(arg_keys[7], (3, 3, 3, C, C), (27 * C) ** -0.5, 0.0625)
    b_one = scatter_about(arg_keys[8], (C,), 0.5, 3.0, (), jnp.float32)
    gain_two = jnp.clip(1.0 + 0.18 * jax.random.normal(arg_keys[9], (C,), jnp.float32), 0.1, 1.9)
    w_two = scatter_about(arg_keys[10], (3, 3, 3, C, C), (27 * C) ** -0.5, 0.0625)
    b_two = scatter_about(arg_keys[11], (C,), 0.5, 3.0, (), jnp.float32)
    return {"latent": latent, "cache_lat": cache_lat, "cache_one": cache_one, "cache_two": cache_two, "w_in": w_in, "b_in": b_in, "gain_one": gain_one, "w_one": w_one, "b_one": b_one, "gain_two": gain_two, "w_two": w_two, "b_two": b_two}


def conv_full(values, cache, kernel, bias):
    frames, height, width, chan = values.shape
    outc = kernel.shape[-1]
    full = jnp.concatenate([cache, values], 0)
    full = jnp.pad(full, ((0, 0), (1, 1), (1, 1), (0, 0)))
    total = jnp.zeros((frames * height * width, outc), jnp.float32)
    for dt in range(3):
        for dy in range(3):
            for dx in range(3):
                window = full[dt:dt + frames, dy:dy + height, dx:dx + width].reshape(-1, chan)
                total = total + jnp.dot(window, kernel[dt, dy, dx], preferred_element_type=jnp.float32)
    return total.reshape(frames, height, width, outc) + bias

def rms_norm(values, gain):
    return values * jax.lax.rsqrt(lax.optimization_barrier(jnp.mean(values * values, -1, keepdims=True)) + 1e-06) * gain

def reference(latent, cache_lat, cache_one, cache_two, w_in, b_in, gain_one, w_one, b_one, gain_two, w_two, b_two):
    first = conv_full(latent, cache_lat, w_in, b_in).astype(jnp.bfloat16)
    normed = jax.nn.silu(rms_norm(first.astype(jnp.float32), gain_one)).astype(jnp.bfloat16)
    middle = conv_full(normed, cache_one, w_one, b_one)
    normed_two = jax.nn.silu(rms_norm(middle, gain_two)).astype(jnp.bfloat16)
    last = conv_full(normed_two, cache_two, w_two, b_two)
    return (first.astype(jnp.float32) + last).astype(jnp.bfloat16)
```

```python
import jax
import jax.numpy as jnp
from jax import lax
from jax.experimental import pallas as pl
from jax.experimental.pallas import tpu as pltpu
from jax.sharding import PartitionSpec as P

BF = jnp.bfloat16
F32 = jnp.float32
MESH = pl.DeviceIdType.MESH
LANE = 128
C = 384
CIN = 16
CHUNK = 256
ROWS = 6
WIDE = ROWS * LANE


def silu(v):
    return v * (0.5 + 0.5 * jnp.tanh(0.5 * v))


def twice(v):
    return jnp.concatenate([v] * (CHUNK // LANE), 1)


def shift_and_add(y):
    pieces = []
    lane = lax.broadcasted_iota(jnp.int32, (C, LANE), 1)
    for b in range(y.shape[1] // LANE):
        s = slice(b * LANE, (b + 1) * LANE)
        left = jnp.where(lane == 0, 0.0, pltpu.roll(y[0:C, s], 1, 1))
        right = jnp.where(lane == LANE - 1, 0.0, pltpu.roll(y[2 * C : 3 * C, s], LANE - 1, 1))
        pieces.append(left + y[C : 2 * C, s] + right)
    return jnp.concatenate(pieces, 1)


def conv_part(source, weights, terms, start):
    x = jnp.concatenate(
        [
            source[slot, :, pl.ds(pl.multiple_of(start + dy * LANE, LANE), CHUNK)]
            for slot, _ in terms
            for dy in range(3)
        ],
        0,
    )
    w = jnp.concatenate(
        [
            jnp.concatenate([weights[dt, dy, dx] for dx in range(3)], 1)
            for _, dt in terms
            for dy in range(3)
        ],
        0,
    )
    y = lax.dot_general(w, x, (((0,), (0,)), ((), ())), preferred_element_type=F32)
    return shift_and_add(y)


def kernel(
    latent,
    cache_lat,
    cache_one,
    cache_two,
    w_in,
    b_in,
    gain_one,
    w_one,
    b_one,
    gain_two,
    w_two,
    b_two,
    out,
    lat,
    latx,
    n1,
    n2,
    h0,
    wv1,
    wv2,
    vec,
    acc,
    stage,
    cstage,
    wsem,
    csem,
    lat_s,
    lat_r,
    cs,
    cr,
    ys,
    yr,
    bs,
    br,
    rs,
    rr,
    osem,
):
    t = lax.axis_index("tm")
    z = lax.axis_index("tile")
    nt = lax.axis_size("tm")
    nz = lax.axis_size("tile")

    def dev(dt, dz):
        return (lax.rem(t + dt + nt, nt), lax.rem(z + dz + nz, nz))

    first_tile = z == 0
    last_tile = z == nz - 1

    barrier = pltpu.get_barrier_semaphore()
    senders = [(-a, b) for a in range(4) for b in (-1, 0, 1) if (a, b) != (0, 0)] + [(1, 0)]
    for a, b in senders:
        pl.semaphore_signal(barrier, inc=1, device_id=dev(a, b), device_id_type=MESH)

    w_copies = []
    for i, (src, dst) in enumerate(((w_one, wv1), (w_two, wv2))):
        for dt in range(3):
            w_copies.append(
                pltpu.make_async_copy(src.at[dt], dst.at[dt], wsem.at[3 * i + dt])
            )
    c_copies = [
        pltpu.make_async_copy(src, cstage.at[i, :, 1:5], csem.at[i])
        for i, src in enumerate((cache_one, cache_two))
    ]

    @pl.when(t <= 1)
    def _():
        c_copies[0].start()

    @pl.when(t == 0)
    def _():
        c_copies[1].start()

    for c in w_copies:
        c.start()

    eye = (
        lax.broadcasted_iota(jnp.int32, (CIN, CIN), 0)
        == lax.broadcasted_iota(jnp.int32, (CIN, CIN), 1)
    ).astype(BF)
    for src, slot in ((latent, 5), (cache_lat, 7)):
        for f in range(2):
            for r in range(4):
                lat[slot + f, 2 + r] = lax.dot_general(
                    eye, src[f, r], (((1,), (1,)), ((), ())), preferred_element_type=F32
                ).astype(BF)

    for i, ref in enumerate((b_in, gain_one, b_one, gain_two, b_two)):
        vec[i] = jnp.transpose(jnp.broadcast_to(ref[...], (LANE, C)))

    pl.semaphore_wait(barrier, len(senders))

    lat_copies = []
    for a, b in [(3, 0), (3, 1), (3, -1), (2, 0), (2, 1), (2, -1), (1, 0), (1, 1), (1, -1), (0, 1), (0, -1)]:
        i = len(lat_copies)
        k0, k1 = (6, 7) if a == 3 else ((5, 9) if a == 0 else (5, 7))
        r0, r1 = {0: (2, 6), 1: (4, 6), -1: (2, 4)}[b]
        lat_copies.append(
            pltpu.make_async_remote_copy(
                src_ref=lat.at[k0:k1, r0:r1],
                dst_ref=lat.at[k0 - 2 * a : k1 - 2 * a, r0 - 4 * b : r1 - 4 * b],
                send_sem=lat_s.at[i],
                recv_sem=lat_r.at[i],
                device_id=dev(a, b),
                device_id_type=MESH,
            )
        )
    for c in lat_copies:
        c.start()

    cache_sends = []
    for i, src in enumerate((cache_one, cache_two)):
        for j, (own, there, dz) in enumerate(((3, 0, 1), (0, 5, -1))):
            cache_sends.append(
                pltpu.make_async_remote_copy(
                    src_ref=src.at[:, own : own + 1],
                    dst_ref=cstage.at[i, :, there : there + 1],
                    send_sem=cs.at[2 * i + j],
                    recv_sem=cr.at[2 * i + j],
                    device_id=dev(0, dz),
                    device_id_type=MESH,
                )
            )

    @pl.when(t <= 1)
    def _():
        cache_sends[0].start()
        cache_sends[1].start()

    @pl.when(t == 0)
    def _():
        cache_sends[2].start()
        cache_sends[3].start()

    def turn(which, target, rows):
        for f in range(2):
            for r in rows:
                target[4 + f, :, r * LANE : (r + 1) * LANE] = jnp.transpose(cstage[which, f, r])

    def blank(target, lo, hi, rows_low, rows_high):
        if rows_low:
            @pl.when(first_tile)
            def _():
                for s in range(lo, hi):
                    target[s, :, 0:LANE] = jnp.zeros((C, LANE), BF)

        if rows_high:
            @pl.when(last_tile)
            def _():
                for s in range(lo, hi):
                    target[s, :, WIDE - LANE : WIDE] = jnp.zeros((C, LANE), BF)

    @pl.when(t <= 1)
    def _():
        c_copies[0].wait()
        turn(0, n1, range(1, 5))

    @pl.when(t == 0)
    def _():
        c_copies[1].wait()
        turn(1, n2, range(1, 5))

    for c in lat_copies:
        c.wait_recv()

    @pl.when(first_tile)
    def _():
        lat[:, 0:2] = jnp.zeros((9, 2, CIN, LANE), BF)

    @pl.when(last_tile)
    def _():
        lat[:, 6:8] = jnp.zeros((9, 2, CIN, LANE), BF)

    def shifts(s, carry):
        v = lat[s].reshape(8 * CIN, LANE).astype(F32)
        lane = lax.broadcasted_iota(jnp.int32, (8 * CIN, LANE), 1)
        left = jnp.where(lane == 0, 0.0, pltpu.roll(v, 1, 1)).astype(BF)
        right = jnp.where(lane == LANE - 1, 0.0, pltpu.roll(v, LANE - 1, 1)).astype(BF)
        latx[s, :, 0:CIN] = left.reshape(8, CIN, LANE)
        latx[s, :, CIN : 2 * CIN] = lat[s]
        latx[s, :, 2 * CIN : 3 * CIN] = right.reshape(8, CIN, LANE)
        return carry

    lax.fori_loop(0, 9, shifts, 0)

    def project(j):
        first_frame = 2 * t - 3 + j
        slots = []
        for dt in range(3):
            before = 2 * t - 5 + j + dt
            cached = jnp.logical_and(first_frame >= 0, before < 0)
            slots.append(jnp.where(cached, 9 + before, j + dt))
        x = jnp.concatenate(
            [
                jnp.concatenate([latx[slots[dt], r + dy] for dt in range(3) for dy in range(3)], 0)
                for r in range(ROWS)
            ],
            1,
        )
        y = lax.dot_general(w_in[...], x, (((0,), (0,)), ((), ())), preferred_element_type=F32)
        y = (y + jnp.concatenate([vec[0]] * ROWS, 1)).astype(BF)
        h0[j] = y
        return y

    def first_norm(j, carry):
        v = project(j).astype(F32)
        scale = lax.rsqrt(jnp.mean(v * v, 0, keepdims=True) + 1e-06)
        v = v * scale * jnp.concatenate([vec[1]] * ROWS, 1)
        n1[j] = silu(v).astype(BF)
        return carry

    lax.fori_loop(0, 4, first_norm, 0)

    @pl.when(t <= 1)
    def _():
        for c in cache_sends[0:2]:
            c.wait_recv()
        turn(0, n1, (0, 5))

    blank(n1, 0, 6, True, True)

    for c in w_copies[0:3]:
        c.wait()

    def frame_send(f, h):
        lanes = pl.ds(pl.multiple_of(LANE + CHUNK * h, LANE), CHUNK)
        i = jnp.where(f == 0, h, 3 - h)
        return pltpu.make_async_remote_copy(
            src_ref=n2.at[1 + f, :, lanes],
            dst_ref=n2.at[3 - 3 * f, :, lanes],
            send_sem=ys.at[i],
            recv_sem=yr.at[i],
            device_id=dev(2 * f - 1, 0),
            device_id_type=MESH,
        )

    def border_send(f, h):
        i = jnp.where(f == 0, h, 3 - h)
        return pltpu.make_async_remote_copy(
            src_ref=n2.at[1 + f, :, pl.ds(pl.multiple_of(LANE + 3 * LANE * h, LANE), LANE)],
            dst_ref=n2.at[1 + f, :, pl.ds(pl.multiple_of(5 * LANE - 5 * LANE * h, LANE), LANE)],
            send_sem=bs.at[i],
            recv_sem=br.at[i],
            device_id=dev(0, 2 * h - 1),
            device_id_type=MESH,
        )

    start_a = jnp.where(t == 1, 5, 0)
    start_b = jnp.where(t == 0, 4, 1)
    next_b = jnp.where(t == 0, 5, 2)

    def first_conv(i, carry):
        f = i // 2
        h = jnp.where(f == 0, i, 3 - i)
        slots = (
            jnp.where(f == 0, start_a, start_b),
            jnp.where(f == 0, 1, next_b),
            2 + f,
        )
        c1 = conv_part(n1, wv1, [(slots[dt], dt) for dt in range(3)], h * CHUNK)
        c1 = c1 + twice(vec[2])
        scale = lax.rsqrt(jnp.mean(c1 * c1, 0, keepdims=True) + 1e-06)
        v = silu(c1 * scale * twice(vec[3])).astype(BF)
        n2[1 + f, :, pl.ds(pl.multiple_of(LANE + CHUNK * h, LANE), CHUNK)] = v
        frame_send(f, h).start()
        border_send(f, h).start()
        return carry

    lax.fori_loop(0, 4, first_conv, 0)

    project(4)

    for c in w_copies[3:6]:
        c.wait()

    @pl.when(t == 0)
    def _():
        for c in cache_sends[2:4]:
            c.wait_recv()
        turn(1, n2, (0, 5))
        blank(n2, 4, 6, True, True)

    def relay(i, slot, up):
        return pltpu.make_async_remote_copy(
            src_ref=n2.at[slot, :, 4 * LANE : 5 * LANE] if up else n2.at[slot, :, LANE : 2 * LANE],
            dst_ref=n2.at[slot, :, 0:LANE] if up else n2.at[slot, :, 5 * LANE : 6 * LANE],
            send_sem=rs.at[i],
            recv_sem=rr.at[i],
            device_id=dev(0, 1 if up else -1),
            device_id_type=MESH,
        )

    relays = [relay(0, 3, False), relay(1, 3, True), relay(2, 0, True), relay(3, 0, False)]
    slot_1 = jnp.where(t == 0, 5, 1)
    slot_0 = jnp.where(t == 0, 4, 0)

    def local_part(i, carry):
        h = i // 2
        o = i % 2

        @pl.when(i == 0)
        def _():
            border_send(0, 1).wait_recv()
            border_send(1, 1).wait_recv()
            blank(n2, 1, 3, True, False)

        @pl.when(i == 2)
        def _():
            border_send(0, 0).wait_recv()
            border_send(1, 0).wait_recv()
            blank(n2, 1, 3, False, True)
            frame_send(0, 0).wait_recv()
            frame_send(0, 1).wait_recv()
            relays[0].start()
            relays[1].start()

        @pl.when(i == 3)
        def _():
            frame_send(1, 1).wait_recv()
            relays[2].start()

        part = conv_part(n2, wv2, [(slot_1, 1 - o), (2, 2 - o)], h * CHUNK)
        acc[o, h] = part
        return carry

    lax.fori_loop(0, 4, local_part, 0)

    def out_copy(o, h):
        return pltpu.make_async_copy(
            stage.at[o, pl.ds(2 * h, 2)], out.at[o, pl.ds(2 * h, 2)], osem.at[2 * o + h]
        )

    def remote_part(i, carry):
        o = 1 - i // 2
        h = i % 2

        @pl.when(i == 0)
        def _():
            relays[1].wait_recv()
            blank(n2, 3, 4, True, False)

        @pl.when(i == 1)
        def _():
            frame_send(1, 0).wait_recv()
            relays[3].start()
            relays[0].wait_recv()
            blank(n2, 3, 4, False, True)

        @pl.when(i == 2)
        def _():
            relays[2].wait_recv()
            blank(n2, 0, 1, True, False)

        @pl.when(i == 3)
        def _():
            relays[3].wait_recv()
            blank(n2, 0, 1, False, True)

        slot = jnp.where(o == 0, slot_0, 3)
        part = conv_part(n2, wv2, [(slot, 2 * o)], h * CHUNK)
        c2 = acc[o, h] + part + twice(vec[4])
        first = h0[3 + o, :, pl.ds(pl.multiple_of(LANE + CHUNK * h, LANE), CHUNK)].astype(F32)
        done = (first + c2).astype(BF)
        for r in range(2):
            stage[o, 2 * h + r] = jnp.transpose(done[:, r * LANE : (r + 1) * LANE])
        out_copy(o, h).start()
        return carry

    lax.fori_loop(0, 4, remote_part, 0)

    for c in lat_copies:
        c.wait_send()

    @pl.when(t <= 1)
    def _():
        for c in cache_sends[0:2]:
            c.wait_send()

    @pl.when(t == 0)
    def _():
        for c in cache_sends[2:4]:
            c.wait_send()

    for f in range(2):
        for h in range(2):
            frame_send(f, h).wait_send()
            border_send(f, h).wait_send()
    for c in relays:
        c.wait_send()
    for o in range(2):
        for h in range(2):
            out_copy(o, h).wait()


def on_device(
    latent,
    cache_lat,
    cache_one,
    cache_two,
    w_in,
    b_in,
    gain_one,
    w_one,
    b_one,
    gain_two,
    w_two,
    b_two,
):
    vmem = pl.BlockSpec(memory_space=pltpu.VMEM)
    hbm = pl.BlockSpec(memory_space=pl.ANY)
    dma = pltpu.SemaphoreType.DMA
    return pl.pallas_call(
        kernel,
        name="decoder_block",
        out_shape=jax.ShapeDtypeStruct((2, 4, LANE, C), BF),
        in_specs=[vmem, vmem, hbm, hbm, vmem, vmem, vmem, hbm, vmem, vmem, hbm, vmem],
        out_specs=hbm,
        scratch_shapes=[
            pltpu.VMEM((9, 8, CIN, LANE), BF),
            pltpu.VMEM((9, 8, 3 * CIN, LANE), BF),
            pltpu.VMEM((6, C, WIDE), BF),
            pltpu.VMEM((6, C, WIDE), BF),
            pltpu.VMEM((5, C, WIDE), BF),
            pltpu.VMEM((3, 3, 3, C, C), BF),
            pltpu.VMEM((3, 3, 3, C, C), BF),
            pltpu.VMEM((5, C, LANE), F32),
            pltpu.VMEM((2, 2, C, CHUNK), F32),
            pltpu.VMEM((2, 4, LANE, C), BF),
            pltpu.VMEM((2, 2, ROWS, LANE, C), BF),
            dma((6,)),
            dma((2,)),
            dma((11,)),
            dma((11,)),
            dma((4,)),
            dma((4,)),
            dma((4,)),
            dma((4,)),
            dma((4,)),
            dma((4,)),
            dma((4,)),
            dma((4,)),
            dma((4,)),
        ],
        compiler_params=pltpu.CompilerParams(
            collective_id=0, has_side_effects=True, vmem_limit_bytes=60 << 20
        ),
    )(
        latent,
        cache_lat,
        cache_one,
        cache_two,
        w_in.reshape(27 * CIN, C),
        b_in[None],
        gain_one[None],
        w_one,
        b_one[None],
        gain_two[None],
        w_two,
        b_two[None],
    )


def solution(mesh):
    return jax.shard_map(
        on_device,
        mesh=mesh,
        in_specs=(
            P("tm", "tile", None, None),
            P(None, "tile", None, None),
            P(None, "tile", None, None),
            P(None, "tile", None, None),
            P(),
            P(),
            P(),
            P(),
            P(),
            P(),
            P(),
            P(),
        ),
        out_specs=P("tm", "tile", None, None),
        check_vma=False,
    )
```

```python
import jax
import jax.numpy as jnp
from jax import lax
from jax.experimental import pallas as pl
from jax.experimental.pallas import tpu as pltpu
from jax.sharding import PartitionSpec as P

BF = jnp.bfloat16
F32 = jnp.float32
MESH = pl.DeviceIdType.MESH
LANE = 128
C = 384
CIN = 16
CHUNK = 256
ROWS = 6
WIDE = ROWS * LANE


def silu(v):
    return v * (0.5 + 0.5 * jnp.tanh(0.5 * v))


def twice(v):
    return jnp.concatenate([v] * (CHUNK // LANE), 1)


def shift_and_add(y):
    pieces = []
    lane = lax.broadcasted_iota(jnp.int32, (C, LANE), 1)
    for b in range(y.shape[1] // LANE):
        s = slice(b * LANE, (b + 1) * LANE)
        left = jnp.where(lane == 0, 0.0, pltpu.roll(y[0:C, s], 1, 1))
        right = jnp.where(lane == LANE - 1, 0.0, pltpu.roll(y[2 * C : 3 * C, s], LANE - 1, 1))
        pieces.append(left + y[C : 2 * C, s] + right)
    return jnp.concatenate(pieces, 1)


def conv_part(source, weights, terms, start):
    x = jnp.concatenate(
        [
            source[slot, :, pl.ds(pl.multiple_of(start + dy * LANE, LANE), CHUNK)]
            for slot, _ in terms
            for dy in range(3)
        ],
        0,
    )
    w = jnp.concatenate(
        [
            jnp.concatenate([weights[dt, dy, dx] for dx in range(3)], 1)
            for _, dt in terms
            for dy in range(3)
        ],
        0,
    )
    y = lax.dot_general(w, x, (((0,), (0,)), ((), ())), preferred_element_type=F32)
    return shift_and_add(y)


def kernel(
    latent,
    cache_lat,
    cache_one,
    cache_two,
    w_in,
    b_in,
    gain_one,
    w_one,
    b_one,
    gain_two,
    w_two,
    b_two,
    out,
    lat,
    latx,
    n1,
    n2,
    h0,
    wv1,
    wv2,
    vec,
    acc,
    stage,
    cstage,
    wsem,
    csem,
    lat_s,
    lat_r,
    cs,
    cr,
    ys,
    yr,
    bs,
    br,
    rs,
    rr,
    osem,
):
    t = lax.axis_index("tm")
    z = lax.axis_index("tile")
    nt = lax.axis_size("tm")
    nz = lax.axis_size("tile")

    def dev(dt, dz):
        return (lax.rem(t + dt + nt, nt), lax.rem(z + dz + nz, nz))

    first_tile = z == 0
    last_tile = z == nz - 1

    barrier = pltpu.get_barrier_semaphore()
    senders = [(-a, b) for a in range(4) for b in (-1, 0, 1) if (a, b) != (0, 0)] + [(1, 0)]
    for a, b in senders:
        pl.semaphore_signal(barrier, inc=1, device_id=dev(a, b), device_id_type=MESH)

    w_copies = []
    for i, (src, dst) in enumerate(((w_one, wv1), (w_two, wv2))):
        for dt in range(3):
            w_copies.append(
                pltpu.make_async_copy(src.at[dt], dst.at[dt], wsem.at[3 * i + dt])
            )
    c_copies = [
        pltpu.make_async_copy(src, cstage.at[i, :, 1:5], csem.at[i])
        for i, src in enumerate((cache_one, cache_two))
    ]

    @pl.when(t <= 1)
    def _():
        c_copies[0].start()

    @pl.when(t == 0)
    def _():
        c_copies[1].start()

    for c in w_copies:
        c.start()

    for src, slot in ((latent, 5), (cache_lat, 7)):
        lat[slot : slot + 2, 2:6] = src[...]

    for i, ref in enumerate((b_in, gain_one, b_one, gain_two, b_two)):
        vec[i] = jnp.transpose(jnp.broadcast_to(ref[...].reshape(1, C), (LANE, C)))

    pl.semaphore_wait(barrier, len(senders))

    lat_copies = []
    for a, b in [(3, 0), (3, 1), (3, -1), (2, 0), (2, 1), (2, -1), (1, 0), (1, 1), (1, -1), (0, 1), (0, -1)]:
        i = len(lat_copies)
        k0, k1 = (6, 7) if a == 3 else ((5, 9) if a == 0 else (5, 7))
        r0, r1 = {0: (2, 6), 1: (4, 6), -1: (2, 4)}[b]
        lat_copies.append(
            pltpu.make_async_remote_copy(
                src_ref=lat.at[k0:k1, r0:r1],
                dst_ref=lat.at[k0 - 2 * a : k1 - 2 * a, r0 - 4 * b : r1 - 4 * b],
                send_sem=lat_s.at[i],
                recv_sem=lat_r.at[i],
                device_id=dev(a, b),
                device_id_type=MESH,
            )
        )
    for c in lat_copies:
        c.start()

    cache_sends = []
    for i, src in enumerate((cache_one, cache_two)):
        for j, (own, there, dz) in enumerate(((3, 0, 1), (0, 5, -1))):
            cache_sends.append(
                pltpu.make_async_remote_copy(
                    src_ref=src.at[:, own : own + 1],
                    dst_ref=cstage.at[i, :, there : there + 1],
                    send_sem=cs.at[2 * i + j],
                    recv_sem=cr.at[2 * i + j],
                    device_id=dev(0, dz),
                    device_id_type=MESH,
                )
            )

    @pl.when(t <= 1)
    def _():
        cache_sends[0].start()
        cache_sends[1].start()

    @pl.when(t == 0)
    def _():
        cache_sends[2].start()
        cache_sends[3].start()

    def turn(which, target, rows):
        for f in range(2):
            for r in rows:
                target[4 + f, :, r * LANE : (r + 1) * LANE] = jnp.transpose(cstage[which, f, r])

    def blank(target, lo, hi, rows_low, rows_high):
        if rows_low:
            @pl.when(first_tile)
            def _():
                for s in range(lo, hi):
                    target[s, :, 0:LANE] = jnp.zeros((C, LANE), BF)

        if rows_high:
            @pl.when(last_tile)
            def _():
                for s in range(lo, hi):
                    target[s, :, WIDE - LANE : WIDE] = jnp.zeros((C, LANE), BF)

    @pl.when(t <= 1)
    def _():
        c_copies[0].wait()
        turn(0, n1, range(1, 5))

    @pl.when(t == 0)
    def _():
        c_copies[1].wait()
        turn(1, n2, range(1, 5))

    for c in lat_copies:
        c.wait_recv()

    @pl.when(first_tile)
    def _():
        lat[:, 0:2] = jnp.zeros((9, 2, CIN, LANE), BF)

    @pl.when(last_tile)
    def _():
        lat[:, 6:8] = jnp.zeros((9, 2, CIN, LANE), BF)

    def shifts(s, carry):
        v = lat[s].reshape(8 * CIN, LANE).astype(F32)
        lane = lax.broadcasted_iota(jnp.int32, (8 * CIN, LANE), 1)
        left = jnp.where(lane == 0, 0.0, pltpu.roll(v, 1, 1)).astype(BF)
        right = jnp.where(lane == LANE - 1, 0.0, pltpu.roll(v, LANE - 1, 1)).astype(BF)
        latx[s, :, 0:CIN] = left.reshape(8, CIN, LANE)
        latx[s, :, CIN : 2 * CIN] = lat[s]
        latx[s, :, 2 * CIN : 3 * CIN] = right.reshape(8, CIN, LANE)
        return carry

    lax.fori_loop(0, 9, shifts, 0)

    def project(j):
        first_frame = 2 * t - 3 + j
        slots = []
        for dt in range(3):
            before = 2 * t - 5 + j + dt
            cached = jnp.logical_and(first_frame >= 0, before < 0)
            slots.append(jnp.where(cached, 9 + before, j + dt))
        x = jnp.concatenate(
            [
                jnp.concatenate([latx[slots[dt], r + dy] for dt in range(3) for dy in range(3)], 0)
                for r in range(ROWS)
            ],
            1,
        )
        y = lax.dot_general(w_in[...], x, (((0,), (0,)), ((), ())), preferred_element_type=F32)
        y = (y + jnp.concatenate([vec[0]] * ROWS, 1)).astype(BF)
        h0[j] = y
        return y

    def first_norm(j, carry):
        v = project(j).astype(F32)
        scale = lax.rsqrt(jnp.mean(v * v, 0, keepdims=True) + 1e-06)
        v = v * scale * jnp.concatenate([vec[1]] * ROWS, 1)
        n1[j] = silu(v).astype(BF)
        return carry

    lax.fori_loop(0, 4, first_norm, 0)

    @pl.when(t <= 1)
    def _():
        for c in cache_sends[0:2]:
            c.wait_recv()
        turn(0, n1, (0, 5))

    blank(n1, 0, 6, True, True)

    for c in w_copies[0:3]:
        c.wait()

    def frame_send(f, h):
        lanes = pl.ds(pl.multiple_of(LANE + CHUNK * h, LANE), CHUNK)
        i = jnp.where(f == 0, h, 3 - h)
        return pltpu.make_async_remote_copy(
            src_ref=n2.at[1 + f, :, lanes],
            dst_ref=n2.at[3 - 3 * f, :, lanes],
            send_sem=ys.at[i],
            recv_sem=yr.at[i],
            device_id=dev(2 * f - 1, 0),
            device_id_type=MESH,
        )

    def border_send(f, h):
        i = jnp.where(f == 0, h, 3 - h)
        return pltpu.make_async_remote_copy(
            src_ref=n2.at[1 + f, :, pl.ds(pl.multiple_of(LANE + 3 * LANE * h, LANE), LANE)],
            dst_ref=n2.at[1 + f, :, pl.ds(pl.multiple_of(5 * LANE - 5 * LANE * h, LANE), LANE)],
            send_sem=bs.at[i],
            recv_sem=br.at[i],
            device_id=dev(0, 2 * h - 1),
            device_id_type=MESH,
        )

    start_a = jnp.where(t == 1, 5, 0)
    start_b = jnp.where(t == 0, 4, 1)
    next_b = jnp.where(t == 0, 5, 2)

    def first_conv(i, carry):
        f = i // 2
        h = jnp.where(f == 0, i, 3 - i)
        slots = (
            jnp.where(f == 0, start_a, start_b),
            jnp.where(f == 0, 1, next_b),
            2 + f,
        )
        c1 = conv_part(n1, wv1, [(slots[dt], dt) for dt in range(3)], h * CHUNK)
        c1 = c1 + twice(vec[2])
        scale = lax.rsqrt(jnp.mean(c1 * c1, 0, keepdims=True) + 1e-06)
        v = silu(c1 * scale * twice(vec[3])).astype(BF)
        n2[1 + f, :, pl.ds(pl.multiple_of(LANE + CHUNK * h, LANE), CHUNK)] = v
        frame_send(f, h).start()
        border_send(f, h).start()
        return carry

    lax.fori_loop(0, 4, first_conv, 0)

    project(4)

    for c in w_copies[3:6]:
        c.wait()

    @pl.when(t == 0)
    def _():
        for c in cache_sends[2:4]:
            c.wait_recv()
        turn(1, n2, (0, 5))
        blank(n2, 4, 6, True, True)

    def relay(i, slot, up):
        return pltpu.make_async_remote_copy(
            src_ref=n2.at[slot, :, 4 * LANE : 5 * LANE] if up else n2.at[slot, :, LANE : 2 * LANE],
            dst_ref=n2.at[slot, :, 0:LANE] if up else n2.at[slot, :, 5 * LANE : 6 * LANE],
            send_sem=rs.at[i],
            recv_sem=rr.at[i],
            device_id=dev(0, 1 if up else -1),
            device_id_type=MESH,
        )

    relays = [relay(0, 3, False), relay(1, 3, True), relay(2, 0, True), relay(3, 0, False)]
    slot_1 = jnp.where(t == 0, 5, 1)
    slot_0 = jnp.where(t == 0, 4, 0)

    def local_part(i, carry):
        h = i // 2
        o = i % 2

        @pl.when(i == 0)
        def _():
            border_send(0, 1).wait_recv()
            border_send(1, 1).wait_recv()
            blank(n2, 1, 3, True, False)

        @pl.when(i == 2)
        def _():
            border_send(0, 0).wait_recv()
            border_send(1, 0).wait_recv()
            blank(n2, 1, 3, False, True)
            frame_send(0, 0).wait_recv()
            frame_send(0, 1).wait_recv()
            relays[0].start()
            relays[1].start()

        @pl.when(i == 3)
        def _():
            frame_send(1, 1).wait_recv()
            relays[2].start()

        part = conv_part(n2, wv2, [(slot_1, 1 - o), (2, 2 - o)], h * CHUNK)
        acc[o, h] = part
        return carry

    lax.fori_loop(0, 4, local_part, 0)

    def out_copy(o, h):
        return pltpu.make_async_copy(
            stage.at[o, pl.ds(2 * h, 2)], out.at[o, pl.ds(2 * h, 2)], osem.at[2 * o + h]
        )

    def remote_part(i, carry):
        o = 1 - i // 2
        h = i % 2

        @pl.when(i == 0)
        def _():
            relays[1].wait_recv()
            blank(n2, 3, 4, True, False)

        @pl.when(i == 1)
        def _():
            frame_send(1, 0).wait_recv()
            relays[3].start()
            relays[0].wait_recv()
            blank(n2, 3, 4, False, True)

        @pl.when(i == 2)
        def _():
            relays[2].wait_recv()
            blank(n2, 0, 1, True, False)

        @pl.when(i == 3)
        def _():
            relays[3].wait_recv()
            blank(n2, 0, 1, False, True)

        slot = jnp.where(o == 0, slot_0, 3)
        part = conv_part(n2, wv2, [(slot, 2 * o)], h * CHUNK)
        c2 = acc[o, h] + part + twice(vec[4])
        first = h0[3 + o, :, pl.ds(pl.multiple_of(LANE + CHUNK * h, LANE), CHUNK)].astype(F32)
        done = (first + c2).astype(BF)
        for r in range(2):
            stage[o, 2 * h + r] = jnp.transpose(done[:, r * LANE : (r + 1) * LANE])
        out_copy(o, h).start()
        return carry

    lax.fori_loop(0, 4, remote_part, 0)

    for c in lat_copies:
        c.wait_send()

    @pl.when(t <= 1)
    def _():
        for c in cache_sends[0:2]:
            c.wait_send()

    @pl.when(t == 0)
    def _():
        for c in cache_sends[2:4]:
            c.wait_send()

    for f in range(2):
        for h in range(2):
            frame_send(f, h).wait_send()
            border_send(f, h).wait_send()
    for c in relays:
        c.wait_send()
    for o in range(2):
        for h in range(2):
            out_copy(o, h).wait()


def on_device(
    latent,
    cache_lat,
    cache_one,
    cache_two,
    w_in,
    b_in,
    gain_one,
    w_one,
    b_one,
    gain_two,
    w_two,
    b_two,
):
    vmem = pl.BlockSpec(memory_space=pltpu.VMEM)
    hbm = pl.BlockSpec(memory_space=pl.ANY)
    dma = pltpu.SemaphoreType.DMA
    return pl.pallas_call(
        kernel,
        name="decoder_block",
        out_shape=jax.ShapeDtypeStruct((2, 4, LANE, C), BF),
        in_specs=[vmem, vmem, hbm, hbm, vmem, vmem, vmem, hbm, vmem, vmem, hbm, vmem],
        out_specs=hbm,
        scratch_shapes=[
            pltpu.VMEM((9, 8, CIN, LANE), BF),
            pltpu.VMEM((9, 8, 3 * CIN, LANE), BF),
            pltpu.VMEM((6, C, WIDE), BF),
            pltpu.VMEM((6, C, WIDE), BF),
            pltpu.VMEM((5, C, WIDE), BF),
            pltpu.VMEM((3, 3, 3, C, C), BF),
            pltpu.VMEM((3, 3, 3, C, C), BF),
            pltpu.VMEM((5, C, LANE), F32),
            pltpu.VMEM((2, 2, C, CHUNK), F32),
            pltpu.VMEM((2, 4, LANE, C), BF),
            pltpu.VMEM((2, 2, ROWS, LANE, C), BF),
            dma((6,)),
            dma((2,)),
            dma((11,)),
            dma((11,)),
            dma((4,)),
            dma((4,)),
            dma((4,)),
            dma((4,)),
            dma((4,)),
            dma((4,)),
            dma((4,)),
            dma((4,)),
            dma((4,)),
        ],
        compiler_params=pltpu.CompilerParams(
            collective_id=0, has_side_effects=True, vmem_limit_bytes=60 << 20
        ),
    )(
        jnp.swapaxes(latent, 2, 3),
        jnp.swapaxes(cache_lat, 2, 3),
        cache_one,
        cache_two,
        w_in.reshape(27 * CIN, C),
        b_in,
        gain_one,
        w_one,
        b_one,
        gain_two,
        w_two,
        b_two,
    )


def solution(mesh):
    return jax.shard_map(
        on_device,
        mesh=mesh,
        in_specs=(
            P("tm", "tile", None, None),
            P(None, "tile", None, None),
            P(None, "tile", None, None),
            P(None, "tile", None, None),
            P(),
            P(),
            P(),
            P(),
            P(),
            P(),
            P(),
            P(),
        ),
        out_specs=P("tm", "tile", None, None),
        check_vma=False,
    )
```
